32 devices in a mesh: ent: 32 (over z, y, x, core).
Axes of the slice: x: 2, y: 2, z: 4, core: 2. Of those that a mesh axis runs over, the one named last changes fastest.
Arguments:
- mentions: bfloat16 [32768, 768], P('ent'), may hold values from -6 to 6
- table: bfloat16 [131072, 768], P('ent'), may hold values from -2 to 2
- picks: int32 [32, 8], P('ent'), may hold values from 0 to 15
- gold: int32 [32768], P('ent'), may hold values from 0 to 2047
Outputs:
- loss: float32 [], replicated
- d_mentions: float32 [32768, 768], P('ent')
- d_table: float32 [131072, 768], P('ent')
The draws below stay inside these ranges and needn't reach their ends.
All inputs are finite; a program needn't handle non-finite values.
Results may differ from the reference program's by a relative error of at most 0.002.
Values may be sent and summed in bfloat16 or wider, within the bound.
No kernel may reach another device: no remote copies, remote signals or barrier semaphores. Data moves between devices by JAX's collectives and lax.ppermute only.
A program may use at most 128 MiB of HBM per device.

```python
import jax
import jax.numpy as jnp
from jax import lax

D = 768
ENT_DEV = 4096
BLK = 256
ROUNDS = 8
MEN = 1024
BPD = 16
CAND = 2048
ENTITIES = 131072
MENTIONS = 32768
N_ENT = 32


def shared_sign(key):
    sign_key = jax.random.fold_in(key, 7301)
    flips = jax.random.bernoulli(sign_key, 0.5, (D,))
    return jnp.where(flips, 1.0, -1.0).astype(jnp.float32)


def draw_mentions(key, part):
    base = jax.random.fold_in(key, 1101)
    k_bulk = jax.random.fold_in(base, 2)
    k_pos = jax.random.fold_in(base, 3)
    k_extra = jax.random.fold_in(base, 4)
    k_mag = jax.random.fold_in(base, 5)
    bulk = jnp.clip(jax.random.normal(k_bulk, (MENTIONS, D), jnp.float32), -5.0, 5.0)
    rows = jnp.arange(MENTIONS, dtype=jnp.int32)
    within = rows % MEN
    device = rows // MEN
    position = jax.random.randint(k_pos, (MENTIONS // MEN,), 0, MEN, dtype=jnp.int32)
    chosen = within == jnp.take(position, device)
    extra = jax.random.randint(k_extra, (MENTIONS,), 0, 16, dtype=jnp.int32) == 0
    magnitude = jnp.where(chosen, 6.0, jax.random.uniform(k_mag, (MENTIONS,), jnp.float32, 4.0, 6.0))
    planted = shared_sign(key)[None, :] * magnitude[:, None]
    aligned = jnp.logical_or(chosen, extra)
    return jnp.where(aligned[:, None], planted, bulk).astype(jnp.bfloat16)


def draw_table(key, part):
    base = jax.random.fold_in(key, 2203)
    k_level = jax.random.fold_in(base, 1)
    k_drop = jax.random.fold_in(base, 2)
    k_bulk = jax.random.fold_in(base, 4)
    nblock = ENTITIES // BLK
    rows = jnp.arange(ENTITIES, dtype=jnp.int32)
    within = rows % BLK
    block = rows // BLK
    strength = jax.random.uniform(k_level, (nblock,), jnp.float32, 45.0, 67.0)
    lowered = jax.random.uniform(k_drop, (nblock,), jnp.float32, 0.3, 0.45)
    level = jnp.take(strength, block) - jnp.where(within == 1, jnp.take(lowered, block), 0.0)
    columns = jnp.arange(D, dtype=jnp.int32)
    alternate = jnp.where(columns % 2 == 0, 0.5, -0.5).astype(jnp.float32)
    profile = jnp.where(within[:, None] == 0, 1.0 + alternate[None, :], 1.0 - alternate[None, :])
    planted = shared_sign(key)[None, :] * profile * (level / jnp.float32(D))[:, None]
    inverse_root = 1.0 / jnp.sqrt(jnp.float32(D))
    bulk = jnp.clip(jax.random.normal(k_bulk, (ENTITIES, D), jnp.float32), -4.0, 4.0) * inverse_root
    return jnp.where((within < 2)[:, None], planted, bulk).astype(jnp.bfloat16)


def with_ends(array, stream_key, least, largest):
    spot = [jax.random.randint(jax.random.fold_in(stream_key, axis), (), 0, length) for axis, length in enumerate(array.shape)]
    widest = array.shape.index(max(array.shape))
    next_to = spot[:widest] + [(spot[widest] + 1) % array.shape[widest]] + spot[widest + 1:]
    return array.at[tuple(spot)].set(least).at[tuple(next_to)].set(largest)


def setup_inputs(seed: int = 0) -> dict:
    key_list = jax.random.split(jax.random.key(seed), 5)
    mentions = draw_mentions(jax.random.fold_in(key_list[4], 71), 0)
    table = draw_table(jax.random.fold_in(key_list[4], 71), 0)
    picks = with_ends(jax.random.randint(key_list[2], (N_ENT, ROUNDS), 0, BPD), jax.random.fold_in(key_list[2], 1), 0, BPD - 1).astype(jnp.int32)
    gold = with_ends(jax.random.randint(key_list[3], (MENTIONS,), 0, CAND), jax.random.fold_in(key_list[3], 1), 0, CAND - 1).astype(jnp.int32)
    return dict(mentions=mentions, table=table, picks=picks, gold=gold)


def reference(mentions, table, picks, gold):
    stride = N_ENT // ROUNDS
    offsets = jnp.arange(ROUNDS, dtype=jnp.int32) * stride + 1
    devices = jnp.arange(N_ENT, dtype=jnp.int32)
    owners = (devices[:, None] - offsets[None, :]) % N_ENT
    chosen = picks[owners, jnp.arange(ROUNDS, dtype=jnp.int32)[None, :]]
    starts = owners * ENT_DEV + chosen * BLK
    rows_all = (starts[:, :, None] + jnp.arange(BLK, dtype=jnp.int32)[None, None, :]).reshape(N_ENT, CAND).astype(jnp.int32)
    ment = mentions.reshape(N_ENT, MEN, D)
    golds = gold.reshape(N_ENT, MEN)

    def step(carry, inputs):
        grads, total = carry
        ment_i, gold_i, rows_i = inputs
        cand = table[rows_i]
        scores = jnp.dot(ment_i, cand.T, preferred_element_type=jnp.float32)
        top = jnp.max(scores, axis=1, keepdims=True)
        lse = top[:, 0] + jnp.log(jnp.sum(jnp.exp(scores - top), axis=1))
        target = jnp.take_along_axis(scores, gold_i[:, None], axis=1)[:, 0]
        total = total + jnp.sum(lse - target)
        onehot = (jnp.arange(CAND, dtype=jnp.int32)[None, :] == gold_i[:, None]).astype(jnp.float32)
        dscore = (jnp.exp(scores - lse[:, None]) - onehot).astype(jnp.bfloat16)
        dment = jnp.dot(dscore, cand, preferred_element_type=jnp.float32)
        dcand = jnp.dot(dscore.T, ment_i, preferred_element_type=jnp.float32)
        grads = grads.at[rows_i].add(dcand)
        return (grads, total), dment

    init = (jnp.zeros((ENTITIES, D), jnp.float32), jnp.zeros((), jnp.float32))
    (grads, total), dments = lax.scan(step, init, (ment, golds, rows_all))
    loss = total / jnp.float32(MENTIONS)
    return (loss, dments.reshape(MENTIONS, D), grads)
```

```python
import math

import jax
import jax.numpy as jnp
from jax import lax
from jax.sharding import PartitionSpec as P

BLK = 256
ROUNDS = 8


FAR_FIRST = (4, 3, 5, 2, 6, 1, 7, 0)
NEAR_FIRST = FAR_FIRST[::-1]


def from_behind(value, axis, by):
    length = lax.axis_size(axis)
    return lax.ppermute(value, axis, [(i, (i + by) % length) for i in range(length)])


def total_over(value, axis):
    length = lax.axis_size(axis)
    step = 1
    while step < length:
        value = value + lax.ppermute(value, axis, [(i, i ^ step) for i in range(length)])
        step *= 2
    return value


def on_device(mentions, table, picks, gold):
    count = lax.axis_size("ent")
    stride = count // ROUNDS
    men, width = mentions.shape
    scale = 2.0 ** math.floor(math.log2(65504.0 / (6.0 * men)))
    cand = {}
    for j in FAR_FIRST:
        block = lax.dynamic_slice(table, (picks[0, j] * BLK, 0), (BLK, width))
        cand[j] = from_behind(block, "ent", j * stride + 1)
    scores, tops, sums, targets = {}, {}, {}, {}
    rows = lax.broadcasted_iota(jnp.int32, (BLK, men), 0)
    for j in NEAR_FIRST:
        s = lax.dot_general(
            cand[j], mentions, (((1,), (1,)), ((), ())), preferred_element_type=jnp.float32
        )
        top = jnp.max(s, axis=0, keepdims=True)
        e = jnp.exp(s - top)
        scores[j], tops[j] = e, top
        sums[j] = jnp.sum(e, axis=0, keepdims=True)
        targets[j] = jnp.sum(
            jnp.where(rows + j * BLK == gold[None, :], s, 0.0), axis=0, keepdims=True
        )
    top = tops[0]
    for j in range(1, ROUNDS):
        top = jnp.maximum(top, tops[j])
    total = sum(sums[j] * jnp.exp(tops[j] - top) for j in range(ROUNDS))
    target = sum(targets[j] for j in range(ROUNDS))
    lse = top + jnp.log(total)
    inverse = 1.0 / total
    dscore, returned = {}, {}
    for j in FAR_FIRST:
        onehot = (rows + j * BLK == gold[None, :]).astype(jnp.float32)
        p = scores[j] * (jnp.exp(tops[j] - top) * inverse)
        dscore[j] = (p - onehot).astype(jnp.bfloat16)
        grad = jnp.dot(dscore[j], mentions, preferred_element_type=jnp.float32)
        returned[j] = from_behind((grad * scale).astype(jnp.float16), "ent", -(j * stride + 1))
    partial_loss = jnp.sum(lse - target)
    loss = total_over(partial_loss, "ent") / jnp.float32(count * men)
    all_dscore = jnp.concatenate([dscore[j] for j in range(ROUNDS)], axis=0)
    all_cand = jnp.concatenate([cand[j] for j in range(ROUNDS)], axis=0)
    d_mentions = lax.dot_general(
        all_dscore, all_cand, (((0,), (0,)), ((), ())), preferred_element_type=jnp.float32
    )
    d_table = jnp.zeros(table.shape, jnp.float32)
    for j in NEAR_FIRST:
        at = (picks[0, j] * BLK, 0)
        held = lax.dynamic_slice(d_table, at, (BLK, width))
        grad = returned[j].astype(jnp.float32) * (1.0 / scale)
        d_table = lax.dynamic_update_slice(d_table, held + grad, at)
    return (loss, d_mentions, d_table)


def solution(mesh):
    return jax.shard_map(
        on_device,
        mesh=mesh,
        in_specs=(P("ent", None), P("ent", None), P("ent", None), P("ent")),
        out_specs=(P(), P("ent", None), P("ent", None)),
        check_vma=False,
    )
```
